32 devices in a mesh: tm: 8 (over z, x), rows: 4 (over y, core).
Axes of the slice: x: 2, y: 2, z: 4, core: 2. Of those that a mesh axis runs over, the one named last changes fastest.
Arguments:
- latents: bfloat16 [32, 16, 32, 256], P('tm', 'rows'), may hold values from -6 to 6
- frame_gaps: float32 [32], P('tm'), may hold values from 0.5 to 250
- decay_rates: float32 [2, 256], replicated, may hold values from 0.0011 to 0.05
- input_kernel: bfloat16 [2, 3, 3, 256, 256], replicated, may hold values from -0.125 to 0.125
- output_kernel: bfloat16 [2, 3, 3, 256, 256], replicated, may hold values from -0.125 to 0.125
- feedthrough: float32 [2, 256], replicated, may hold values from -1 to 1
Outputs:
- encoded: bfloat16 [32, 16, 32, 256], P('tm', 'rows')
The draws below stay inside these ranges and needn't reach their ends.
All inputs are finite; a program needn't handle non-finite values.
Results may differ from the reference program's by a relative error of at most 0.012.
Values may be sent and summed in bfloat16 or wider, within the bound.
A program may use at most 64 MiB of HBM per device.

```python
import math
import jax
import jax.numpy as jnp
from jax import lax

C = 256
P_SIZE = 256
W = 32
STACK_COUNT = 2
FRAMES = 32
H = 16


def draw_frame_gaps(key, part):
    key_parent, seed_occurrences, key_positions = jax.random.split(jax.random.fold_in(key, 11), 3)
    snapshot_spacing = jnp.exp(jax.random.uniform(key_parent, (FRAMES,), jnp.float32, -0.69, 0.69))
    occurrence_locations = jax.random.permutation(key_positions, FRAMES)[:2]
    rapid_occurrences = jax.random.uniform(seed_occurrences, (2,), jnp.float32, 150.0, 250.0)
    return snapshot_spacing.at[occurrence_locations].set(rapid_occurrences)


def permute_channels(key_layer):
    return jax.random.permutation(key_layer, P_SIZE)


def draw_decay_rates(key, part):
    key_pick, key_fast, key_slow = jax.random.split(jax.random.fold_in(key, 23), 3)
    fast_rates = jax.random.uniform(key_fast, (STACK_COUNT, P_SIZE), jnp.float32, 0.03, 0.05)
    slow_rates = jnp.exp(jax.random.uniform(key_slow, (STACK_COUNT, P_SIZE), jnp.float32, math.log(0.0012), math.log(0.0024)))
    ranking = jax.vmap(permute_channels)(jax.random.split(key_pick, STACK_COUNT))
    quick_tally = P_SIZE // 2
    chosen_fast = ranking < quick_tally
    return jnp.where(chosen_fast, fast_rates, slow_rates)


def block_scale(stream_key, dims, cuts, smallest, high):
    loudness, own = 1.0, jax.random.fold_in(stream_key, 6)
    for position, blocks in cuts:
        steps = jnp.exp(jax.random.uniform(jax.random.fold_in(own, position), (blocks,), jnp.float32, smallest / len(cuts), high / len(cuts)))
        loudness = loudness * jnp.repeat(steps, dims[position] // blocks).reshape([-1 if axis == position else 1 for axis in range(len(dims))])
    return loudness


def centred(key, shape, deviation, most, cuts=(), dtype=jnp.bfloat16):
    entries = deviation * jax.random.normal(key, shape, jnp.float32)
    if cuts:
        entries = entries * block_scale(key, shape, cuts, -0.22, 0.18)
    return jnp.clip(entries, -most, most).astype(dtype)


def setup_inputs(seed: int = 0) -> dict:
    streams_of = jax.random.split(jax.random.key(seed), 7)
    return {
        "latents": centred(streams_of[0], (FRAMES, H, W, C), 1.0, 6.0, ((0, 8), (1, 4))),
        "frame_gaps": draw_frame_gaps(jax.random.fold_in(streams_of[6], 71), 0),
        "decay_rates": draw_decay_rates(jax.random.fold_in(streams_of[6], 71), 0),
        "input_kernel": centred(streams_of[3], (STACK_COUNT, 3, 3, C, P_SIZE), (9 * C) ** -0.5, 0.125),
        "output_kernel": centred(streams_of[4], (STACK_COUNT, 3, 3, P_SIZE, C), (9 * P_SIZE) ** -0.5, 0.125),
        "feedthrough": jnp.clip(jax.random.uniform(streams_of[5], (STACK_COUNT, C), jnp.float32, -1.0, 1.0), -1.0, 1.0),
    }


def convolve(inputs, kernel):
    frames, vertical_extent, columns, channels = inputs.shape
    padded = jnp.pad(inputs, ((0, 0), (1, 1), (1, 1), (0, 0)))
    summed = jnp.zeros((frames * vertical_extent * columns, kernel.shape[-1]), jnp.float32)
    for row_tap in range(3):
        for col_tap in range(3):
            window = padded[:, row_tap:row_tap + vertical_extent, col_tap:col_tap + columns, :].reshape(-1, channels)
            summed = summed + jnp.dot(window, kernel[row_tap, col_tap], preferred_element_type=jnp.float32)
    return summed.reshape(frames, vertical_extent, columns, -1)

def recurrence(driving, decays):

    def advance(carried, pieces):
        driven, factor = pieces
        carried = factor * carried + jnp.sqrt(1.0 - factor * factor) * driven
        return (carried, carried)
    initial = jnp.zeros(driving.shape[1:], jnp.float32)
    _, states = lax.scan(advance, initial, (driving, decays))
    return states

def reference(latents, frame_gaps, decay_rates, input_kernel, output_kernel, feedthrough):
    inputs = latents
    for layer_index in range(STACK_COUNT):
        decays = jnp.exp(-frame_gaps[:, None] * decay_rates[layer_index][None, :])
        driving = convolve(inputs, input_kernel[layer_index])
        states = recurrence(driving, decays).astype(jnp.bfloat16)
        premix = convolve(states, output_kernel[layer_index]) + feedthrough[layer_index] * inputs.astype(jnp.float32)
        inputs = jax.nn.gelu(premix, approximate=True).astype(jnp.bfloat16)
    return inputs
```

```python
import functools

import jax
import jax.numpy as jnp
from jax import lax
from jax.experimental import pallas as pl
from jax.experimental.pallas import tpu as pltpu
from jax.sharding import PartitionSpec as P

MESH = pl.DeviceIdType.MESH
F32 = jnp.float32
BF16 = jnp.bfloat16


def gelu(v):
    return 0.5 * v * (1.0 + jnp.tanh(0.7978845608028654 * (v + 0.044715 * (v * v * v))))


def fold(v):
    half = v.shape[-1] // 2
    return jnp.concatenate([v[..., :half], v[..., half:]], axis=-2)


def unfold(v):
    half = v.shape[-2] // 2
    return jnp.concatenate([v[..., :half, :], v[..., half:, :]], axis=-1)


def kernel(
    n, bands, base, owners,
    lat, gaps_in, rates_in, feed_in, win, wout,
    out,
    gaps, rates, feed, x0, x1, xs, xh, st, sth, halo, wbuf, cums, dec_src, dec_box,
    fin, inbox, xbox, outbox, carry, hcarry,
    small_sem, lat_sem, w_sem, halo_send, halo_recv, dec_send, dec_recv, fin_send, fin_recv, cross_send, cross_recv,
    car_send, car_recv, hcar_send, hcar_recv,
):
    layers = win.shape[0]
    frames, rows, width, chans = lat.shape
    share = width // owners
    me = lax.axis_index("tm")
    band = lax.axis_index("rows")
    has_up = band > 0
    has_down = band < bands - 1
    is_owner = jnp.logical_and(me >= base, me < base + owners)
    my_share = lax.rem(me + owners * n - base, owners)
    groups = [list(range(rows // 2)), list(range(rows // 2, rows))]
    sides = [(has_up, lax.rem(band + bands - 1, bands)), (has_down, lax.rem(band + 1, bands))]
    beyond_row = [-1, rows]
    edge_row = [0, rows - 1]
    pending = []

    def both(*conds):
        return functools.reduce(jnp.logical_and, conds)

    def send(cond, src, dst, ssem, rsem, dev):
        copy = pltpu.make_async_remote_copy(
            src_ref=src, dst_ref=dst, send_sem=ssem, recv_sem=rsem, device_id=dev, device_id_type=MESH
        )
        pl.when(cond)(copy.start)
        pending.append((cond, copy))

    def receive(cond, dst, ssem, rsem, dev):
        copy = pltpu.make_async_remote_copy(
            src_ref=dst, dst_ref=dst, send_sem=ssem, recv_sem=rsem, device_id=dev, device_id_type=MESH
        )
        pl.when(cond)(copy.wait_recv)

    barrier = pltpu.get_barrier_semaphore()

    def greet(cond, dev):
        @pl.when(cond)
        def _():
            pl.semaphore_signal(barrier, inc=1, device_id=dev, device_id_type=MESH)

    small = [pltpu.make_async_copy(src, dst, small_sem.at[i])
             for i, (src, dst) in enumerate(((gaps_in, gaps), (rates_in, rates), (feed_in, feed)))]
    w_copies = {(layer, which): pltpu.make_async_copy(src.at[layer], wbuf.at[layer, which], w_sem.at[layer, which])
                for layer in range(layers) for which, src in enumerate((win, wout))}
    row_copies = [pltpu.make_async_copy(lat.at[:, r], x0.at[r], lat_sem.at[r]) for r in range(rows)]

    for k in range(n):
        owns = base <= k < base + owners
        greet(me != k if owns else both(is_owner, me != k), {"tm": k})
    for copy in small:
        copy.start()
    w_copies[0, 0].start()
    for copy in row_copies:
        copy.start()
    for there, other in sides:
        for k in range(n):
            if base <= k < base + owners:
                greet(there, {"tm": k, "rows": other})
            else:
                greet(both(there, jnp.logical_or(is_owner, me == k)), {"tm": k, "rows": other})

    for d, (there, _other) in enumerate(sides):
        @pl.when(jnp.logical_not(there))
        def _():
            for layer in range(layers):
                for which in range(2):
                    halo[layer, which, d] = jnp.zeros(halo.shape[3:], BF16)
                xbox[layer, d] = jnp.zeros(xbox.shape[2:], BF16)

        @pl.when(jnp.logical_or(me == 0, jnp.logical_not(there)))
        def _():
            for layer in range(layers):
                hcarry[layer, d] = jnp.zeros(hcarry.shape[2:], BF16)

    @pl.when(me == 0)
    def _():
        carry[...] = jnp.zeros(carry.shape, BF16)

    for copy in small:
        copy.wait()
    decays = []
    for layer in range(layers):
        rate = rates[layer : layer + 1, :]
        factors = [jnp.exp(-gaps[t] * rate) for t in range(frames)]
        total = factors[0]
        cums[layer, 0:1, :] = total
        for t in range(1, frames):
            total = total * factors[t]
            cums[layer, t : t + 1, :] = total
        dec_src[layer : layer + 1, :] = total
        decays.append([(factor, jnp.sqrt(1.0 - factor * factor)) for factor in factors])

    @pl.when(is_owner)
    def _():
        dec_box[me] = dec_src[...]

    neighbours = has_up.astype(jnp.int32) + has_down.astype(jnp.int32)

    def meet():
        pl.semaphore_wait(
            barrier, jnp.where(is_owner, n - 1 + neighbours * n, owners + neighbours * (owners + 1))
        )

    def send_halo(layer, which, top, bottom):
        for d, (src, (there, other)) in enumerate(zip((top, bottom), sides)):
            send(there, src, halo.at[layer, which, 1 - d], halo_send.at[layer, which, d],
                 halo_recv.at[layer, which, 1 - d], {"rows": other})

    def wait_halo(layer, which):
        for d, (there, other) in enumerate(sides):
            receive(there, halo.at[layer, which, d], halo_send.at[layer, which, d],
                    halo_recv.at[layer, which, d], {"rows": other})

    def spread(parts, count):
        size = count * frames * width
        column = lax.rem(lax.broadcasted_iota(jnp.int32, (size, parts[0].shape[1]), 0), width)
        left = jnp.where(column == 0, 0.0, pltpu.roll(parts[0], 1, 0))
        right = jnp.where(column == width - 1, 0.0, pltpu.roll(parts[2], size - 1, 0))
        return (parts[1] + left + right).reshape(count, frames, width, -1)

    def conv(x, weights, wanted):
        lhs = [jnp.concatenate([x(i + a - 1).reshape(frames * width, chans) for i in wanted], axis=0) for a in range(3)]
        lhs = jnp.concatenate(lhs, axis=1)
        parts = []
        for b in range(3):
            rhs = jnp.concatenate([weights(a, b) for a in range(3)], axis=0)
            parts.append(jnp.dot(lhs, rhs, preferred_element_type=F32))
        return spread(parts, len(wanted))

    def scan(layer, driven):
        states = []
        for t in range(frames):
            factor, gain = decays[layer][t]
            fresh = gain * driven[t]
            states.append(fresh if t == 0 else factor * states[-1] + fresh)
        return states

    def drive(x, layer, g):
        mine = groups[g]
        wanted = [-1] + mine if g == 0 else mine + [rows]
        nothing = jnp.zeros((frames, width, chans), BF16)
        driven = conv(lambda i: x(i) if 0 <= i < rows else nothing, lambda a, b: wbuf[layer, 0, a, b], wanted)
        for j, r in enumerate(wanted):
            states = scan(layer, driven[j])
            if 0 <= r < rows:
                for t in range(frames):
                    st[r, t] = states[t]
            slot = r - mine[0] if 0 <= r < rows else len(mine)
            for s in range(owners):
                fin[layer, g, s, slot] = fold(states[-1][s * share : (s + 1) * share]).astype(BF16)

    def send_fin(layer, g):
        count = len(groups[g])
        there, other = sides[g]
        for s in range(owners):
            @pl.when(me == base + s)
            def _():
                inbox[layer, g, me, :count] = fin[layer, g, s, :count]

            send(both(me < n - 1, there), fin.at[layer, g, s, count], xbox.at[layer, 1 - g, me],
                 cross_send.at[layer, g, s], cross_recv.at[layer, 1 - g, me], {"tm": base + s, "rows": other})
            send(both(me < n - 1, me != base + s), fin.at[layer, g, s, :count], inbox.at[layer, g, me, :count],
                 fin_send.at[layer, g, s], fin_recv.at[layer, g, me], {"tm": base + s})

    def own(layer, g):
        count = len(groups[g])
        there, other = sides[g]
        edge = 0 if g == 0 else count - 1
        total = None
        for k in range(1, n):
            receive(both(is_owner, me != k - 1), inbox.at[layer, g, k - 1, :count], fin_send.at[layer, g, 0],
                    fin_recv.at[layer, g, k - 1], {"tm": k - 1})
            receive(both(is_owner, there), xbox.at[layer, g, k - 1], cross_send.at[layer, g, 0],
                    cross_recv.at[layer, g, k - 1], {"tm": k - 1, "rows": other})
            if layer == 0 and g == 0:
                receive(both(is_owner, me != k - 1), dec_box.at[k - 1], dec_send.at[0], dec_recv.at[k - 1], {"tm": k - 1})
            last = unfold(inbox[layer, g, k - 1, :count].astype(F32))
            cross = unfold(xbox[layer, g, k - 1].astype(F32))
            last = jnp.stack([last[j] + cross if j == edge else last[j] for j in range(count)])
            total = last if total is None else dec_box[k - 1, layer : layer + 1, :] * total + last
            outbox[layer, g, k, :count] = fold(total).astype(BF16)
            send(both(is_owner, there), outbox.at[layer, g, k, edge], hcarry.at[layer, 1 - g, my_share],
                 hcar_send.at[layer, g, k], hcar_recv.at[layer, 1 - g, my_share], {"tm": k, "rows": other})
            send(both(is_owner, me != k), outbox.at[layer, g, k, :count], carry.at[layer, g, my_share, :count],
                 car_send.at[layer, g, k], car_recv.at[layer, g, my_share], {"tm": k})

            @pl.when(both(is_owner, me == k))
            def _():
                carry[layer, g, my_share, :count] = outbox[layer, g, k, :count]

    def complete(layer):
        wait_halo(layer, 0)
        for d in range(2):
            v = halo[layer, 0, d].reshape(frames * width, chans)
            parts = [jnp.dot(v, wbuf[layer, 0, 2 * d, b], preferred_element_type=F32) for b in range(3)]
            states = scan(layer, spread(parts, 1)[0])
            for t in range(frames):
                state = st[edge_row[d], t] + states[t]
                st[edge_row[d], t] = state
                sth[layer, d, t] = state.astype(BF16)
        send_halo(layer, 1, sth.at[layer, 0], sth.at[layer, 1])

    def finish(layer, g):
        count = len(groups[g])
        for s in range(owners):
            receive(both(me > 0, me != base + s), carry.at[layer, g, s, :count], car_send.at[layer, g, 0],
                    car_recv.at[layer, g, s], {"tm": base + s})
        for j, r in enumerate(groups[g]):
            incoming = jnp.concatenate([unfold(carry[layer, g, s, j].astype(F32)) for s in range(owners)], axis=0)
            for t in range(frames):
                xs[layer, r, t] = (st[r, t] + cums[layer, t : t + 1, :] * incoming).astype(BF16)

    def finish_halo(layer):
        wait_halo(layer, 1)
        for d, (there, other) in enumerate(sides):
            for s in range(owners):
                receive(both(me > 0, there), hcarry.at[layer, d, s], hcar_send.at[layer, d, 0],
                        hcar_recv.at[layer, d, s], {"tm": base + s, "rows": other})
            incoming = jnp.concatenate([unfold(hcarry[layer, d, s].astype(F32)) for s in range(owners)], axis=0)
            for t in range(frames):
                local = halo[layer, 1, d, t].astype(F32)
                xh[layer, d, t] = (local + cums[layer, t : t + 1, :] * incoming).astype(BF16)

    def mix(x, layer, wanted, put):
        def states(i):
            return xh[layer, 0] if i < 0 else xh[layer, 1] if i == rows else xs[layer, i]

        mixed = conv(states, lambda a, b: wbuf[layer, 1, a, b], wanted)
        gain = feed[layer : layer + 1, :]
        for j, r in enumerate(wanted):
            skipped = x(r).astype(F32)
            put(r, gelu(mixed[j] + gain * skipped).astype(BF16))

    x = lambda r: x0[r]
    for copy in row_copies:
        copy.wait()
    for layer in range(layers):
        if layer == 0:
            w_copies[0, 0].wait()
            w_copies[0, 1].start()
            drive(x, layer, 0)
            meet()
            send_halo(0, 0, lat.at[:, 0], lat.at[:, rows - 1])
            for s in range(owners):
                send(both(me < n - 1, me != base + s), dec_src, dec_box.at[me], dec_send.at[s],
                     dec_recv.at[me], {"tm": base + s})
            send_fin(layer, 0)
        else:
            w_copies[layer, 0].wait()
            send_halo(layer, 0, x1.at[layer - 1, 0], x1.at[layer - 1, rows - 1])
            drive(x, layer, 0)
            send_fin(layer, 0)
        drive(x, layer, 1)
        send_fin(layer, 1)
        if layer < layers - 1:
            w_copies[layer + 1, 0].start()
            w_copies[layer + 1, 1].start()
        complete(layer)
        for g in range(2):
            own(layer, g)
        for g in range(2):
            finish(layer, g)
        finish_halo(layer)
        w_copies[layer, 1].wait()
        if layer == layers - 1:
            def put(r, v):
                out[:, r] = v
        else:
            def put(r, v):
                x1[layer, r] = v

        mix(x, layer, list(range(rows)), put)
        x = functools.partial(lambda layer, r: x1[layer, r], layer)

    for cond, copy in pending:
        pl.when(cond)(copy.wait_send)


def per_device(n, bands, latents, frame_gaps, decay_rates, input_kernel, output_kernel, feedthrough):
    frames, rows, width, chans = latents.shape
    layers = input_kernel.shape[0]
    owners = min(n // 2, max(width // 8, 1))
    base = n // 2 - owners // 2
    share = width // owners
    most = rows - rows // 2
    hbm = pl.BlockSpec(memory_space=pltpu.HBM)
    vmem = pl.BlockSpec(memory_space=pltpu.VMEM)
    dma = pltpu.SemaphoreType.DMA
    return pl.pallas_call(
        functools.partial(kernel, n, bands, base, owners),
        out_shape=pltpu.VMEM(latents.shape, BF16),
        in_specs=[hbm] * 6,
        out_specs=vmem,
        scratch_shapes=[
            pltpu.SMEM((frames,), F32),
            pltpu.VMEM((layers, chans), F32),
            pltpu.VMEM((layers, chans), F32),
            pltpu.VMEM((rows, frames, width, chans), BF16),
            pltpu.VMEM((max(layers - 1, 1), rows, frames, width, chans), BF16),
            pltpu.VMEM((layers, rows, frames, width, chans), BF16),
            pltpu.VMEM((layers, 2, frames, width, chans), BF16),
            pltpu.VMEM((rows, frames, width, chans), F32),
            pltpu.VMEM((layers, 2, frames, width, chans), BF16),
            pltpu.VMEM((layers, 2, 2, frames, width, chans), BF16),
            pltpu.VMEM((layers, 2) + input_kernel.shape[1:], BF16),
            pltpu.VMEM((layers, frames, chans), F32),
            pltpu.VMEM((layers, chans), F32),
            pltpu.VMEM((n, layers, chans), F32),
            pltpu.VMEM((layers, 2, owners, most + 1, 2 * share, chans // 2), BF16),
            pltpu.VMEM((layers, 2, n, most, 2 * share, chans // 2), BF16),
            pltpu.VMEM((layers, 2, n, 2 * share, chans // 2), BF16),
            pltpu.VMEM((layers, 2, n, most, 2 * share, chans // 2), BF16),
            pltpu.VMEM((layers, 2, owners, most, 2 * share, chans // 2), BF16),
            pltpu.VMEM((layers, 2, owners, 2 * share, chans // 2), BF16),
            dma((3,)),
            dma((rows,)),
            dma((layers, 2)),
            dma((layers, 2, 2)),
            dma((layers, 2, 2)),
            dma((owners,)),
            dma((n,)),
            dma((layers, 2, owners)),
            dma((layers, 2, n)),
            dma((layers, 2, owners)),
            dma((layers, 2, n)),
            dma((layers, 2, n)),
            dma((layers, 2, owners)),
            dma((layers, 2, n)),
            dma((layers, 2, owners)),
        ],
        compiler_params=pltpu.CompilerParams(collective_id=0, has_side_effects=True, vmem_limit_bytes=60 * 1024 * 1024),
    )(latents, frame_gaps, decay_rates, feedthrough, input_kernel, output_kernel)


def solution(mesh):
    in_specs = (P("tm", "rows", None, None), P("tm"), P(), P(), P(), P())
    out_specs = P("tm", "rows", None, None)
    return jax.shard_map(
        functools.partial(per_device, mesh.shape["tm"], mesh.shape["rows"]),
        mesh=mesh, in_specs=in_specs, out_specs=out_specs, check_vma=False,
    )
```

```python
import functools

import jax
import jax.numpy as jnp
from jax import lax
from jax.experimental import pallas as pl
from jax.experimental.pallas import tpu as pltpu
from jax.sharding import PartitionSpec as P

MESH = pl.DeviceIdType.MESH
F32 = jnp.float32
BF16 = jnp.bfloat16


def gelu(v):
    return 0.5 * v * (1.0 + jnp.tanh(0.7978845608028654 * (v + 0.044715 * (v * v * v))))


def fold(v):
    half = v.shape[-1] // 2
    return jnp.concatenate([v[..., :half], v[..., half:]], axis=-2)


def unfold(v):
    half = v.shape[-2] // 2
    return jnp.concatenate([v[..., :half, :], v[..., half:, :]], axis=-1)


def kernel(
    n, bands, base, owners,
    lat, gaps_in, rates_in, feed_in, win, wout,
    out,
    gaps, rates, feed, x0, x1, xs, xh, st, sth, halo, wbuf, cums, dec_src, dec_box,
    fin, inbox, xbox, outbox, carry, hcarry,
    small_sem, lat_sem, w_sem, halo_send, halo_recv, dec_send, dec_recv, fin_send, fin_recv, cross_send, cross_recv,
    car_send, car_recv, hcar_send, hcar_recv,
):
    layers = win.shape[0]
    frames, rows, width, chans = lat.shape
    share = width // owners
    me = lax.axis_index("tm")
    band = lax.axis_index("rows")
    has_up = band > 0
    has_down = band < bands - 1
    is_owner = jnp.logical_and(me >= base, me < base + owners)
    my_share = lax.rem(me + owners * n - base, owners)
    groups = [list(range(rows // 2)), list(range(rows // 2, rows))]
    sides = [(has_up, lax.rem(band + bands - 1, bands)), (has_down, lax.rem(band + 1, bands))]
    beyond_row = [-1, rows]
    edge_row = [0, rows - 1]

    def both(*conds):
        return functools.reduce(jnp.logical_and, conds)

    def send(cond, src, dst, ssem, rsem, dev):
        copy = pltpu.make_async_remote_copy(
            src_ref=src, dst_ref=dst, send_sem=ssem, recv_sem=rsem, device_id=dev, device_id_type=MESH
        )
        pl.when(cond)(copy.start)

    def waiter(ref, sem):
        return pltpu.make_async_remote_copy(
            src_ref=ref, dst_ref=ref, send_sem=sem, recv_sem=sem, device_id={"tm": 0}, device_id_type=MESH
        )

    def received(cond, ref, sem):
        if ref is not None:
            pl.when(cond)(lambda: waiter(ref, sem).wait_recv())

    def sent(cond, ref, sem):
        if ref is not None:
            pl.when(cond)(lambda: waiter(ref, sem).wait_send())

    def first(ref, lead, size, *rest):
        return ref.at[(*lead, pl.ds(0, size), *rest)] if size else None

    barrier = pltpu.get_barrier_semaphore()

    def greet(cond, dev):
        @pl.when(cond)
        def _():
            pl.semaphore_signal(barrier, inc=1, device_id=dev, device_id_type=MESH)

    small = [pltpu.make_async_copy(src, dst, small_sem.at[i])
             for i, (src, dst) in enumerate(((gaps_in, gaps), (rates_in, rates), (feed_in, feed)))]
    w_copies = {(layer, which): pltpu.make_async_copy(src.at[layer], wbuf.at[layer, which], w_sem.at[layer, which])
                for layer in range(layers) for which, src in enumerate((win, wout))}
    row_copies = [pltpu.make_async_copy(lat.at[:, r], x0.at[r], lat_sem) for r in range(rows)]

    for k in range(n):
        owns = base <= k < base + owners
        greet(me != k if owns else both(is_owner, me != k), {"tm": k})
    for copy in small:
        copy.start()
    w_copies[0, 0].start()
    for copy in row_copies:
        copy.start()
    for there, other in sides:
        for k in range(n):
            if base <= k < base + owners:
                greet(there, {"tm": k, "rows": other})
            else:
                greet(both(there, jnp.logical_or(is_owner, me == k)), {"tm": k, "rows": other})

    for d, (there, _other) in enumerate(sides):
        @pl.when(jnp.logical_not(there))
        def _():
            for layer in range(layers):
                for which in range(2):
                    halo[layer, which, d] = jnp.zeros(halo.shape[3:], BF16)
                xbox[layer, d] = jnp.zeros(xbox.shape[2:], BF16)

        @pl.when(jnp.logical_or(me == 0, jnp.logical_not(there)))
        def _():
            for layer in range(layers):
                hcarry[layer, d] = jnp.zeros(hcarry.shape[2:], BF16)

    @pl.when(me == 0)
    def _():
        carry[...] = jnp.zeros(carry.shape, BF16)

    for copy in small:
        copy.wait()
    decays = []
    for layer in range(layers):
        rate = rates[layer : layer + 1, :]
        factors = [jnp.exp(-gaps[t] * rate) for t in range(frames)]
        total = factors[0]
        cums[layer, 0:1, :] = total
        for t in range(1, frames):
            total = total * factors[t]
            cums[layer, t : t + 1, :] = total
        dec_src[layer : layer + 1, :] = total
        decays.append([(factor, jnp.sqrt(1.0 - factor * factor)) for factor in factors])

    @pl.when(is_owner)
    def _():
        dec_box[me] = dec_src[...]

    neighbours = has_up.astype(jnp.int32) + has_down.astype(jnp.int32)

    def meet():
        pl.semaphore_wait(
            barrier, jnp.where(is_owner, n - 1 + neighbours * n, owners + neighbours * (owners + 1))
        )

    def send_halo(layer, which, top, bottom):
        for d, (src, (there, other)) in enumerate(zip((top, bottom), sides)):
            send(there, src, halo.at[layer, which, 1 - d], halo_send.at[d],
                 halo_recv.at[layer, which, 1 - d], {"rows": other})

    def wait_halo(layer, which):
        for d, (there, _other) in enumerate(sides):
            received(there, halo.at[layer, which, d], halo_recv.at[layer, which, d])

    def spread(parts, count):
        size = count * frames * width
        column = lax.rem(lax.broadcasted_iota(jnp.int32, (size, parts[0].shape[1]), 0), width)
        left = jnp.where(column == 0, 0.0, pltpu.roll(parts[0], 1, 0))
        right = jnp.where(column == width - 1, 0.0, pltpu.roll(parts[2], size - 1, 0))
        return (parts[1] + left + right).reshape(count, frames, width, -1)

    def conv(x, weights, wanted):
        lhs = [jnp.concatenate([x(i + a - 1).reshape(frames * width, chans) for i in wanted], axis=0) for a in range(3)]
        lhs = jnp.concatenate(lhs, axis=1)
        parts = []
        for b in range(3):
            rhs = jnp.concatenate([weights(a, b) for a in range(3)], axis=0)
            parts.append(jnp.dot(lhs, rhs, preferred_element_type=F32))
        return spread(parts, len(wanted))

    def scan(layer, driven):
        states = []
        for t in range(frames):
            factor, gain = decays[layer][t]
            fresh = gain * driven[t]
            states.append(fresh if t == 0 else factor * states[-1] + fresh)
        return states

    def drive(x, layer, g):
        mine = groups[g]
        wanted = [-1] + mine if g == 0 else mine + [rows]
        nothing = jnp.zeros((frames, width, chans), BF16)
        driven = conv(lambda i: x(i) if 0 <= i < rows else nothing, lambda a, b: wbuf[layer, 0, a, b], wanted)
        for j, r in enumerate(wanted):
            states = scan(layer, driven[j])
            if 0 <= r < rows:
                for t in range(frames):
                    st[r, t] = states[t]
            slot = r - mine[0] if 0 <= r < rows else len(mine)
            for s in range(owners):
                fin[layer, g, s, slot] = fold(states[-1][s * share : (s + 1) * share]).astype(BF16)

    def send_fin(layer, g):
        count = len(groups[g])
        there, other = sides[g]
        for s in range(owners):
            @pl.when(me == base + s)
            def _():
                inbox[layer, g, me, :count] = fin[layer, g, s, :count]

            send(both(me < n - 1, there), fin.at[layer, g, s, count], xbox.at[layer, 1 - g, me],
                 cross_send.at[g], cross_recv.at[layer, 1 - g], {"tm": base + s, "rows": other})
            send(both(me < n - 1, me != base + s), fin.at[layer, g, s, :count], inbox.at[layer, g, me, :count],
                 fin_send.at[g], fin_recv.at[layer, g], {"tm": base + s})

    def own(layer, g):
        count = len(groups[g])
        there, other = sides[g]
        edge = 0 if g == 0 else count - 1

        @pl.when(is_owner)
        def _():
            for last, size in ((me < n - 1, n - 2), (me == n - 1, n - 1)):
                received(last, first(inbox, (layer, g), size, pl.ds(0, count)), fin_recv.at[layer, g])
                if layer == 0 and g == 0:
                    received(last, first(dec_box, (), size), dec_recv)
            received(there, first(xbox, (layer, g), n - 1), cross_recv.at[layer, g])
            total = None
            for k in range(1, n):
                last = unfold(inbox[layer, g, k - 1, :count].astype(F32))
                cross = unfold(xbox[layer, g, k - 1].astype(F32))
                last = jnp.stack([last[j] + cross if j == edge else last[j] for j in range(count)])
                total = last if total is None else dec_box[k - 1, layer : layer + 1, :] * total + last
                outbox[layer, g, k, :count] = fold(total).astype(BF16)
                send(there, outbox.at[layer, g, k, edge], hcarry.at[layer, 1 - g, my_share],
                     hcar_send.at[g], hcar_recv.at[layer, 1 - g], {"tm": k, "rows": other})
                send(me != k, outbox.at[layer, g, k, :count], carry.at[layer, g, my_share, :count],
                     car_send.at[g], car_recv.at[layer, g], {"tm": k})

            carry[layer, g, my_share, :count] = outbox[layer, g, me, :count]

    def complete(layer):
        wait_halo(layer, 0)
        for d in range(2):
            v = halo[layer, 0, d].reshape(frames * width, chans)
            parts = [jnp.dot(v, wbuf[layer, 0, 2 * d, b], preferred_element_type=F32) for b in range(3)]
            states = scan(layer, spread(parts, 1)[0])
            for t in range(frames):
                state = st[edge_row[d], t] + states[t]
                st[edge_row[d], t] = state
                sth[layer, d, t] = state.astype(BF16)
        send_halo(layer, 1, sth.at[layer, 0], sth.at[layer, 1])

    def finish(layer, g):
        count = len(groups[g])
        for cond, size in ((is_owner, owners - 1), (jnp.logical_not(is_owner), owners)):
            received(both(me > 0, cond), first(carry, (layer, g), size, pl.ds(0, count)), car_recv.at[layer, g])
        for j, r in enumerate(groups[g]):
            incoming = jnp.concatenate([unfold(carry[layer, g, s, j].astype(F32)) for s in range(owners)], axis=0)
            for t in range(frames):
                xs[layer, r, t] = (st[r, t] + cums[layer, t : t + 1, :] * incoming).astype(BF16)

    def finish_halo(layer):
        wait_halo(layer, 1)
        for d, (there, _other) in enumerate(sides):
            received(both(me > 0, there), hcarry.at[layer, d], hcar_recv.at[layer, d])
            incoming = jnp.concatenate([unfold(hcarry[layer, d, s].astype(F32)) for s in range(owners)], axis=0)
            for t in range(frames):
                local = halo[layer, 1, d, t].astype(F32)
                xh[layer, d, t] = (local + cums[layer, t : t + 1, :] * incoming).astype(BF16)

    def mix(x, layer, wanted, put):
        def states(i):
            return xh[layer, 0] if i < 0 else xh[layer, 1] if i == rows else xs[layer, i]

        mixed = conv(states, lambda a, b: wbuf[layer, 1, a, b], wanted)
        gain = feed[layer : layer + 1, :]
        for j, r in enumerate(wanted):
            skipped = x(r).astype(F32)
            put(r, gelu(mixed[j] + gain * skipped).astype(BF16))

    x = lambda r: x0[r]
    pltpu.make_async_copy(x0, x0, lat_sem).wait()
    for layer in range(layers):
        if layer == 0:
            w_copies[0, 0].wait()
            w_copies[0, 1].start()
            drive(x, layer, 0)
            meet()
            send_halo(0, 0, lat.at[:, 0], lat.at[:, rows - 1])
            for s in range(owners):
                send(both(me < n - 1, me != base + s), dec_src, dec_box.at[me], dec_send,
                     dec_recv, {"tm": base + s})
            send_fin(layer, 0)
        else:
            w_copies[layer, 0].wait()
            send_halo(layer, 0, x1.at[layer - 1, 0], x1.at[layer - 1, rows - 1])
            drive(x, layer, 0)
            send_fin(layer, 0)
        drive(x, layer, 1)
        send_fin(layer, 1)
        if layer < layers - 1:
            w_copies[layer + 1, 0].start()
            w_copies[layer + 1, 1].start()
        complete(layer)
        for g in range(2):
            own(layer, g)
        for g in range(2):
            finish(layer, g)
        finish_halo(layer)
        w_copies[layer, 1].wait()
        if layer == layers - 1:
            def put(r, v):
                out[:, r] = v
        else:
            def put(r, v):
                x1[layer, r] = v

        mix(x, layer, list(range(rows)), put)
        x = functools.partial(lambda layer, r: x1[layer, r], layer)

    for cond, size in ((is_owner, owners - 1), (jnp.logical_not(is_owner), owners)):
        sent(both(me < n - 1, cond), first(dec_box, (), size), dec_send)
        for g in range(2):
            sent(both(me < n - 1, cond), first(fin, (slice(None), g), size, pl.ds(0, len(groups[g]))), fin_send.at[g])
    for g, (there, _other) in enumerate(sides):
        sent(there, halo.at[:, :, g], halo_send.at[g])
        sent(both(me < n - 1, there), fin.at[:, g, :, len(groups[g])], cross_send.at[g])
        sent(is_owner, first(outbox, (slice(None), g), n - 2, pl.ds(0, len(groups[g]))), car_send.at[g])
        sent(both(is_owner, there), outbox.at[:, g, pl.ds(0, n - 1), 0], hcar_send.at[g])


def per_device(n, bands, latents, frame_gaps, decay_rates, input_kernel, output_kernel, feedthrough):
    frames, rows, width, chans = latents.shape
    layers = input_kernel.shape[0]
    owners = min(n // 2, max(width // 8, 1))
    base = n // 2 - owners // 2
    share = width // owners
    most = rows - rows // 2
    hbm = pl.BlockSpec(memory_space=pltpu.HBM)
    vmem = pl.BlockSpec(memory_space=pltpu.VMEM)
    dma = pltpu.SemaphoreType.DMA
    return pl.pallas_call(
        functools.partial(kernel, n, bands, base, owners),
        out_shape=pltpu.VMEM(latents.shape, BF16),
        in_specs=[hbm] * 6,
        out_specs=vmem,
        scratch_shapes=[
            pltpu.SMEM((frames,), F32),
            pltpu.VMEM((layers, chans), F32),
            pltpu.VMEM((layers, chans), F32),
            pltpu.VMEM((rows, frames, width, chans), BF16),
            pltpu.VMEM((max(layers - 1, 1), rows, frames, width, chans), BF16),
            pltpu.VMEM((layers, rows, frames, width, chans), BF16),
            pltpu.VMEM((layers, 2, frames, width, chans), BF16),
            pltpu.VMEM((rows, frames, width, chans), F32),
            pltpu.VMEM((layers, 2, frames, width, chans), BF16),
            pltpu.VMEM((layers, 2, 2, frames, width, chans), BF16),
            pltpu.VMEM((layers, 2) + input_kernel.shape[1:], BF16),
            pltpu.VMEM((layers, frames, chans), F32),
            pltpu.VMEM((layers, chans), F32),
            pltpu.VMEM((n, layers, chans), F32),
            pltpu.VMEM((layers, 2, owners, most + 1, 2 * share, chans // 2), BF16),
            pltpu.VMEM((layers, 2, n, most, 2 * share, chans // 2), BF16),
            pltpu.VMEM((layers, 2, n, 2 * share, chans // 2), BF16),
            pltpu.VMEM((layers, 2, n, most, 2 * share, chans // 2), BF16),
            pltpu.VMEM((layers, 2, owners, most, 2 * share, chans // 2), BF16),
            pltpu.VMEM((layers, 2, owners, 2 * share, chans // 2), BF16),
            dma((3,)),
            dma,
            dma((layers, 2)),
            dma((2,)),
            dma((layers, 2, 2)),
            dma,
            dma,
            dma((2,)),
            dma((layers, 2)),
            dma((2,)),
            dma((layers, 2)),
            dma((2,)),
            dma((layers, 2)),
            dma((2,)),
            dma((layers, 2)),
        ],
        compiler_params=pltpu.CompilerParams(collective_id=0, has_side_effects=True, vmem_limit_bytes=60 * 1024 * 1024),
    )(latents, frame_gaps, decay_rates, feedthrough, input_kernel, output_kernel)


def solution(mesh):
    in_specs = (P("tm", "rows", None, None), P("tm"), P(), P(), P(), P())
    out_specs = P("tm", "rows", None, None)
    return jax.shard_map(
        functools.partial(per_device, mesh.shape["tm"], mesh.shape["rows"]),
        mesh=mesh, in_specs=in_specs, out_specs=out_specs, check_vma=False,
    )
```

```python
import functools

import jax
import jax.numpy as jnp
from jax import lax
from jax.experimental import pallas as pl
from jax.experimental.pallas import tpu as pltpu
from jax.sharding import PartitionSpec as P

MESH = pl.DeviceIdType.MESH
F32 = jnp.float32
BF16 = jnp.bfloat16


def gelu(v):
    return 0.5 * v * (1.0 + jnp.tanh(0.7978845608028654 * (v + 0.044715 * (v * v * v))))


def fold(v):
    half = v.shape[-1] // 2
    return jnp.concatenate([v[..., :half], v[..., half:]], axis=-2)


def unfold(v):
    half = v.shape[-2] // 2
    return jnp.concatenate([v[..., :half, :], v[..., half:, :]], axis=-1)


def kernel(
    n, bands, base, owners,
    lat, gaps_in, rates_in, feed_in, win, wout,
    out,
    gaps, rates, feed, x0, x1, xs, xh, st, sth, halo, wbuf, cums, dec_src, dec_box,
    fin, inbox, xbox, outbox, carry, hcarry,
    small_sem, lat_sem, w_sem, halo_send, halo_recv, dec_send, dec_recv, fin_send, fin_recv, cross_send, cross_recv,
    car_send, car_recv, hcar_send, hcar_recv,
):
    layers = win.shape[0]
    frames, rows, width, chans = lat.shape
    share = width // owners
    me = lax.axis_index("tm")
    band = lax.axis_index("rows")
    has_up = band > 0
    has_down = band < bands - 1
    is_owner = jnp.logical_and(me >= base, me < base + owners)
    my_share = lax.rem(me + owners * n - base, owners)
    groups = [list(range(rows // 2)), list(range(rows // 2, rows))]
    sides = [(has_up, lax.rem(band + bands - 1, bands)), (has_down, lax.rem(band + 1, bands))]
    beyond_row = [-1, rows]
    edge_row = [0, rows - 1]

    def both(*conds):
        return functools.reduce(jnp.logical_and, conds)

    def send(cond, src, dst, ssem, rsem, dev):
        copy = pltpu.make_async_remote_copy(
            src_ref=src, dst_ref=dst, send_sem=ssem, recv_sem=rsem, device_id=dev, device_id_type=MESH
        )
        pl.when(cond)(copy.start)

    def waiter(ref, sem):
        return pltpu.make_async_remote_copy(
            src_ref=ref, dst_ref=ref, send_sem=sem, recv_sem=sem, device_id={"tm": 0}, device_id_type=MESH
        )

    def received(cond, ref, sem):
        if ref is not None:
            pl.when(cond)(lambda: waiter(ref, sem).wait_recv())

    def sent(cond, ref, sem):
        if ref is not None:
            pl.when(cond)(lambda: waiter(ref, sem).wait_send())

    def first(ref, lead, size, *rest):
        return ref.at[(*lead, pl.ds(0, size), *rest)] if size else None

    barrier = pltpu.get_barrier_semaphore()

    def greet(cond, dev):
        @pl.when(cond)
        def _():
            pl.semaphore_signal(barrier, inc=1, device_id=dev, device_id_type=MESH)

    small = [pltpu.make_async_copy(src, dst, small_sem.at[i])
             for i, (src, dst) in enumerate(((gaps_in, gaps), (rates_in, rates), (feed_in, feed)))]
    w_copies = {(layer, which): pltpu.make_async_copy(src.at[layer], wbuf.at[layer, which], w_sem.at[layer, which])
                for layer in range(layers) for which, src in enumerate((win, wout))}
    row_copies = [pltpu.make_async_copy(lat.at[:, r], x0.at[r], lat_sem) for r in range(rows)]

    w_copies[0, 0].start()
    for copy in small:
        copy.start()
    for copy in row_copies:
        copy.start()
    for k in range(n):
        owns = base <= k < base + owners
        greet(me != k if owns else both(is_owner, me != k), {"tm": k})
    for there, other in sides:
        for k in range(n):
            if base <= k < base + owners:
                greet(there, {"tm": k, "rows": other})
            else:
                greet(both(there, jnp.logical_or(is_owner, me == k)), {"tm": k, "rows": other})

    for d, (there, _other) in enumerate(sides):
        @pl.when(jnp.logical_not(there))
        def _():
            for layer in range(layers):
                for which in range(2):
                    halo[layer, which, d] = jnp.zeros(halo.shape[3:], BF16)
                xbox[layer, d] = jnp.zeros(xbox.shape[2:], BF16)

        @pl.when(jnp.logical_or(me == 0, jnp.logical_not(there)))
        def _():
            for layer in range(layers):
                hcarry[layer, d] = jnp.zeros(hcarry.shape[2:], BF16)

    @pl.when(me == 0)
    def _():
        carry[...] = jnp.zeros(carry.shape, BF16)

    for copy in small:
        copy.wait()
    decays = []
    for layer in range(layers):
        rate = rates[layer : layer + 1, :]
        factors = [jnp.exp(-gaps[t] * rate) for t in range(frames)]
        total = factors[0]
        cums[layer, 0:1, :] = total
        for t in range(1, frames):
            total = total * factors[t]
            cums[layer, t : t + 1, :] = total
        dec_src[layer : layer + 1, :] = total
        decays.append([(factor, jnp.sqrt(1.0 - factor * factor)) for factor in factors])

    @pl.when(is_owner)
    def _():
        dec_box[me] = dec_src[...]

    neighbours = has_up.astype(jnp.int32) + has_down.astype(jnp.int32)

    def meet():
        pl.semaphore_wait(
            barrier, jnp.where(is_owner, n - 1 + neighbours * n, owners + neighbours * (owners + 1))
        )

    def send_halo(layer, which, top, bottom):
        for d, (src, (there, other)) in enumerate(zip((top, bottom), sides)):
            send(there, src, halo.at[layer, which, 1 - d], halo_send.at[d],
                 halo_recv.at[layer, which, 1 - d], {"rows": other})

    def wait_halo(layer, which):
        for d, (there, _other) in enumerate(sides):
            received(there, halo.at[layer, which, d], halo_recv.at[layer, which, d])

    def spread(parts, count):
        size = count * frames * width
        column = lax.rem(lax.broadcasted_iota(jnp.int32, (size, parts[0].shape[1]), 0), width)
        left = jnp.where(column == 0, 0.0, pltpu.roll(parts[0], 1, 0))
        right = jnp.where(column == width - 1, 0.0, pltpu.roll(parts[2], size - 1, 0))
        return (parts[1] + left + right).reshape(count, frames, width, -1)

    def conv(x, weights, wanted):
        lhs = [jnp.concatenate([x(i + a - 1).reshape(frames * width, chans) for i in wanted], axis=0) for a in range(3)]
        lhs = jnp.concatenate(lhs, axis=1)
        parts = []
        for b in range(3):
            rhs = jnp.concatenate([weights(a, b) for a in range(3)], axis=0)
            parts.append(jnp.dot(lhs, rhs, preferred_element_type=F32))
        return spread(parts, len(wanted))

    def partial_conv(x, weights, wanted):
        size = frames * width
        blocks = {(a, i): x(i + a - 1).reshape(size, chans) for a in range(3) for i in wanted if 0 <= i + a - 1 < rows}
        full = [i for i in wanted if all((a, i) in blocks for a in range(3))]
        parts = []
        for b in range(3):
            made = {}
            for i in wanted:
                taps = tuple(a for a in range(3) if (a, i) in blocks)
                made.setdefault(taps, []).append(i)
            rows_of = {}
            for taps, which in made.items():
                lhs = jnp.concatenate([jnp.concatenate([blocks[a, i] for i in which], axis=0) for a in taps], axis=1)
                rhs = jnp.concatenate([weights(a, b) for a in taps], axis=0)
                got = jnp.dot(lhs, rhs, preferred_element_type=F32)
                for j, i in enumerate(which):
                    rows_of[i] = got[j * size : (j + 1) * size]
            parts.append(jnp.concatenate([rows_of[i] for i in wanted], axis=0))
        return spread(parts, len(wanted))

    def scan(layer, driven):
        states = []
        for t in range(frames):
            factor, gain = decays[layer][t]
            fresh = gain * driven[t]
            states.append(fresh if t == 0 else factor * states[-1] + fresh)
        return states

    def drive(x, layer, g):
        mine = groups[g]
        wanted = [-1] + mine if g == 0 else mine + [rows]
        driven = partial_conv(x, lambda a, b: wbuf[layer, 0, a, b], wanted)
        for j, r in enumerate(wanted):
            states = scan(layer, driven[j])
            if 0 <= r < rows:
                for t in range(frames):
                    st[r, t] = states[t]
            slot = r - mine[0] if 0 <= r < rows else len(mine)
            for s in range(owners):
                fin[layer, g, s, slot] = fold(states[-1][s * share : (s + 1) * share]).astype(BF16)

    def send_fin(layer, g):
        count = len(groups[g])
        there, other = sides[g]
        for s in range(owners):
            @pl.when(me == base + s)
            def _():
                inbox[layer, g, me, :count] = fin[layer, g, s, :count]

            send(both(me < n - 1, there), fin.at[layer, g, s, count], xbox.at[layer, 1 - g, me],
                 cross_send.at[g], cross_recv.at[layer, 1 - g], {"tm": base + s, "rows": other})
            send(both(me < n - 1, me != base + s), fin.at[layer, g, s, :count], inbox.at[layer, g, me, :count],
                 fin_send.at[g], fin_recv.at[layer, g], {"tm": base + s})

    def own(layer, g):
        count = len(groups[g])
        there, other = sides[g]
        edge = 0 if g == 0 else count - 1

        @pl.when(is_owner)
        def _():
            for last, size in ((me < n - 1, n - 2), (me == n - 1, n - 1)):
                received(last, first(inbox, (layer, g), size, pl.ds(0, count)), fin_recv.at[layer, g])
                if layer == 0 and g == 0:
                    received(last, first(dec_box, (), size), dec_recv)
            received(there, first(xbox, (layer, g), n - 1), cross_recv.at[layer, g])
            total = None
            for k in range(1, n):
                last = unfold(inbox[layer, g, k - 1, :count].astype(F32))
                cross = unfold(xbox[layer, g, k - 1].astype(F32))
                last = jnp.stack([last[j] + cross if j == edge else last[j] for j in range(count)])
                total = last if total is None else dec_box[k - 1, layer : layer + 1, :] * total + last
                outbox[layer, g, k, :count] = fold(total).astype(BF16)
                send(there, outbox.at[layer, g, k, edge], hcarry.at[layer, 1 - g, my_share],
                     hcar_send.at[g], hcar_recv.at[layer, 1 - g], {"tm": k, "rows": other})
                send(me != k, outbox.at[layer, g, k, :count], carry.at[layer, g, my_share, :count],
                     car_send.at[g], car_recv.at[layer, g], {"tm": k})

            carry[layer, g, my_share, :count] = outbox[layer, g, me, :count]

    def complete(layer):
        wait_halo(layer, 0)
        for d in range(2):
            v = halo[layer, 0, d].reshape(frames * width, chans)
            parts = [jnp.dot(v, wbuf[layer, 0, 2 * d, b], preferred_element_type=F32) for b in range(3)]
            states = scan(layer, spread(parts, 1)[0])
            for t in range(frames):
                state = st[edge_row[d], t] + states[t]
                st[edge_row[d], t] = state
                sth[layer, d, t] = state.astype(BF16)
        send_halo(layer, 1, sth.at[layer, 0], sth.at[layer, 1])

    def finish(layer, g):
        count = len(groups[g])
        for cond, size in ((is_owner, owners - 1), (jnp.logical_not(is_owner), owners)):
            received(both(me > 0, cond), first(carry, (layer, g), size, pl.ds(0, count)), car_recv.at[layer, g])
        for j, r in enumerate(groups[g]):
            incoming = jnp.concatenate([unfold(carry[layer, g, s, j].astype(F32)) for s in range(owners)], axis=0)
            for t in range(frames):
                xs[layer, r, t] = (st[r, t] + cums[layer, t : t + 1, :] * incoming).astype(BF16)

    def finish_halo(layer):
        wait_halo(layer, 1)
        for d, (there, _other) in enumerate(sides):
            received(both(me > 0, there), hcarry.at[layer, d], hcar_recv.at[layer, d])
            incoming = jnp.concatenate([unfold(hcarry[layer, d, s].astype(F32)) for s in range(owners)], axis=0)
            for t in range(frames):
                local = halo[layer, 1, d, t].astype(F32)
                xh[layer, d, t] = (local + cums[layer, t : t + 1, :] * incoming).astype(BF16)

    def mix(x, layer, wanted, put):
        def states(i):
            return xh[layer, 0] if i < 0 else xh[layer, 1] if i == rows else xs[layer, i]

        mixed = conv(states, lambda a, b: wbuf[layer, 1, a, b], wanted)
        gain = feed[layer : layer + 1, :]
        for j, r in enumerate(wanted):
            skipped = x(r).astype(F32)
            put(r, gelu(mixed[j] + gain * skipped).astype(BF16))

    x = lambda r: x0[r]
    pltpu.make_async_copy(x0, x0, lat_sem).wait()
    for layer in range(layers):
        if layer == 0:
            w_copies[0, 0].wait()
            w_copies[0, 1].start()
            drive(x, layer, 0)
            drive(x, layer, 1)
            meet()
            send_halo(0, 0, lat.at[:, 0], lat.at[:, rows - 1])
            for s in range(owners):
                send(both(me < n - 1, me != base + s), dec_src, dec_box.at[me], dec_send,
                     dec_recv, {"tm": base + s})
            send_fin(layer, 0)
        else:
            w_copies[layer, 0].wait()
            send_halo(layer, 0, x1.at[layer - 1, 0], x1.at[layer - 1, rows - 1])
            drive(x, layer, 0)
            send_fin(layer, 0)
            drive(x, layer, 1)
        send_fin(layer, 1)
        if layer < layers - 1:
            w_copies[layer + 1, 0].start()
            w_copies[layer + 1, 1].start()
        complete(layer)
        for g in range(2):
            own(layer, g)
        for g in range(2):
            finish(layer, g)
        finish_halo(layer)
        w_copies[layer, 1].wait()
        if layer == layers - 1:
            def put(r, v):
                out[:, r] = v
        else:
            def put(r, v):
                x1[layer, r] = v

        mix(x, layer, list(range(rows)), put)
        x = functools.partial(lambda layer, r: x1[layer, r], layer)

    for cond, size in ((is_owner, owners - 1), (jnp.logical_not(is_owner), owners)):
        sent(both(me < n - 1, cond), first(dec_box, (), size), dec_send)
        for g in range(2):
            sent(both(me < n - 1, cond), first(fin, (slice(None), g), size, pl.ds(0, len(groups[g]))), fin_send.at[g])
    for g, (there, _other) in enumerate(sides):
        sent(there, halo.at[:, :, g], halo_send.at[g])
        sent(both(me < n - 1, there), fin.at[:, g, :, len(groups[g])], cross_send.at[g])
        sent(is_owner, first(outbox, (slice(None), g), n - 2, pl.ds(0, len(groups[g]))), car_send.at[g])
        sent(both(is_owner, there), outbox.at[:, g, pl.ds(0, n - 1), 0], hcar_send.at[g])


def per_device(n, bands, latents, frame_gaps, decay_rates, input_kernel, output_kernel, feedthrough):
    frames, rows, width, chans = latents.shape
    layers = input_kernel.shape[0]
    owners = min(n // 2, max(width // 8, 1))
    base = n // 2 - owners // 2
    share = width // owners
    most = rows - rows // 2
    hbm = pl.BlockSpec(memory_space=pltpu.HBM)
    vmem = pl.BlockSpec(memory_space=pltpu.VMEM)
    dma = pltpu.SemaphoreType.DMA
    return pl.pallas_call(
        functools.partial(kernel, n, bands, base, owners),
        out_shape=pltpu.VMEM(latents.shape, BF16),
        in_specs=[hbm] * 6,
        out_specs=vmem,
        scratch_shapes=[
            pltpu.SMEM((frames,), F32),
            pltpu.VMEM((layers, chans), F32),
            pltpu.VMEM((layers, chans), F32),
            pltpu.VMEM((rows, frames, width, chans), BF16),
            pltpu.VMEM((max(layers - 1, 1), rows, frames, width, chans), BF16),
            pltpu.VMEM((layers, rows, frames, width, chans), BF16),
            pltpu.VMEM((layers, 2, frames, width, chans), BF16),
            pltpu.VMEM((rows, frames, width, chans), F32),
            pltpu.VMEM((layers, 2, frames, width, chans), BF16),
            pltpu.VMEM((layers, 2, 2, frames, width, chans), BF16),
            pltpu.VMEM((layers, 2) + input_kernel.shape[1:], BF16),
            pltpu.VMEM((layers, frames, chans), F32),
            pltpu.VMEM((layers, chans), F32),
            pltpu.VMEM((n, layers, chans), F32),
            pltpu.VMEM((layers, 2, owners, most + 1, 2 * share, chans // 2), BF16),
            pltpu.VMEM((layers, 2, n, most, 2 * share, chans // 2), BF16),
            pltpu.VMEM((layers, 2, n, 2 * share, chans // 2), BF16),
            pltpu.VMEM((layers, 2, n, most, 2 * share, chans // 2), BF16),
            pltpu.VMEM((layers, 2, owners, most, 2 * share, chans // 2), BF16),
            pltpu.VMEM((layers, 2, owners, 2 * share, chans // 2), BF16),
            dma((3,)),
            dma,
            dma((layers, 2)),
            dma((2,)),
            dma((layers, 2, 2)),
            dma,
            dma,
            dma((2,)),
            dma((layers, 2)),
            dma((2,)),
            dma((layers, 2)),
            dma((2,)),
            dma((layers, 2)),
            dma((2,)),
            dma((layers, 2)),
        ],
        compiler_params=pltpu.CompilerParams(collective_id=0, has_side_effects=True, vmem_limit_bytes=60 * 1024 * 1024),
    )(latents, frame_gaps, decay_rates, feedthrough, input_kernel, output_kernel)


def solution(mesh):
    in_specs = (P("tm", "rows", None, None), P("tm"), P(), P(), P(), P())
    out_specs = P("tm", "rows", None, None)
    return jax.shard_map(
        functools.partial(per_device, mesh.shape["tm"], mesh.shape["rows"]),
        mesh=mesh, in_specs=in_specs, out_specs=out_specs, check_vma=False,
    )
```

```python
import functools

import jax
import jax.numpy as jnp
from jax import lax
from jax.experimental import pallas as pl
from jax.experimental.pallas import tpu as pltpu
from jax.sharding import PartitionSpec as P

MESH = pl.DeviceIdType.MESH
F32 = jnp.float32
BF16 = jnp.bfloat16


def gelu(v):
    return 0.5 * v * (1.0 + jnp.tanh(0.7978845608028654 * (v + 0.044715 * (v * v * v))))


def fold(v):
    half = v.shape[-1] // 2
    return jnp.concatenate([v[..., :half], v[..., half:]], axis=-2)


def unfold(v):
    half = v.shape[-2] // 2
    return jnp.concatenate([v[..., :half, :], v[..., half:, :]], axis=-1)


def kernel(
    n, bands, base, owners,
    lat, gaps_in, rates_in, feed_in, win, wout,
    out,
    gaps, rates, feed, x0, x1, xs, xh, st, sth, halo, wbuf, cums, dec_src, dec_box,
    fin, inbox, xbox, outbox, carry, hcarry,
    small_sem, lat_sem, w_sem, halo_send, halo_recv, dec_send, dec_recv, fin_send, fin_recv, cross_send, cross_recv,
    car_send, car_recv, hcar_send, hcar_recv,
):
    layers = win.shape[0]
    frames, rows, width, chans = lat.shape
    share = width // owners
    me = lax.axis_index("tm")
    band = lax.axis_index("rows")
    has_up = band > 0
    has_down = band < bands - 1
    is_owner = jnp.logical_and(me >= base, me < base + owners)
    my_share = lax.rem(me + owners * n - base, owners)
    groups = [list(range(rows // 2)), list(range(rows // 2, rows))]
    sides = [(has_up, lax.rem(band + bands - 1, bands)), (has_down, lax.rem(band + 1, bands))]
    beyond_row = [-1, rows]
    edge_row = [0, rows - 1]

    def both(*conds):
        return functools.reduce(jnp.logical_and, conds)

    def send(cond, src, dst, ssem, rsem, dev):
        copy = pltpu.make_async_remote_copy(
            src_ref=src, dst_ref=dst, send_sem=ssem, recv_sem=rsem, device_id=dev, device_id_type=MESH
        )
        pl.when(cond)(copy.start)

    def waiter(ref, sem):
        return pltpu.make_async_remote_copy(
            src_ref=ref, dst_ref=ref, send_sem=sem, recv_sem=sem, device_id={"tm": 0}, device_id_type=MESH
        )

    def received(cond, ref, sem):
        if ref is not None:
            pl.when(cond)(lambda: waiter(ref, sem).wait_recv())

    def sent(cond, ref, sem):
        if ref is not None:
            pl.when(cond)(lambda: waiter(ref, sem).wait_send())

    def first(ref, lead, size, *rest):
        return ref.at[(*lead, pl.ds(0, size), *rest)] if size else None

    barrier = pltpu.get_barrier_semaphore()

    def greet(cond, dev):
        @pl.when(cond)
        def _():
            pl.semaphore_signal(barrier, inc=1, device_id=dev, device_id_type=MESH)

    small = [pltpu.make_async_copy(src, dst, small_sem.at[i])
             for i, (src, dst) in enumerate(((gaps_in, gaps), (rates_in, rates), (feed_in, feed)))]
    w_copies = {(layer, which): pltpu.make_async_copy(src.at[layer], wbuf.at[layer, which], w_sem.at[layer, which])
                for layer in range(layers) for which, src in enumerate((win, wout))}
    row_copies = [pltpu.make_async_copy(lat.at[:, r], x0.at[r], lat_sem) for r in range(rows)]

    for k in range(n):
        owns = base <= k < base + owners
        greet(me != k if owns else both(is_owner, me != k), {"tm": k})
    for copy in small:
        copy.start()
    w_copies[0, 0].start()
    for copy in row_copies:
        copy.start()
    for there, other in sides:
        for k in range(n):
            if base <= k < base + owners:
                greet(there, {"tm": k, "rows": other})
            else:
                greet(both(there, jnp.logical_or(is_owner, me == k)), {"tm": k, "rows": other})

    for d, (there, _other) in enumerate(sides):
        @pl.when(jnp.logical_not(there))
        def _():
            for layer in range(layers):
                for which in range(2):
                    halo[layer, which, d] = jnp.zeros(halo.shape[3:], BF16)
                xbox[layer, d] = jnp.zeros(xbox.shape[2:], BF16)

        @pl.when(jnp.logical_or(me == 0, jnp.logical_not(there)))
        def _():
            for layer in range(layers):
                hcarry[layer, d] = jnp.zeros(hcarry.shape[2:], BF16)

    @pl.when(me == 0)
    def _():
        carry[...] = jnp.zeros(carry.shape, BF16)

    for copy in small:
        copy.wait()
    decays = []
    for layer in range(layers):
        rate = rates[layer : layer + 1, :]
        factors = [jnp.exp(-gaps[t] * rate) for t in range(frames)]
        total = factors[0]
        cums[layer, 0:1, :] = total
        for t in range(1, frames):
            total = total * factors[t]
            cums[layer, t : t + 1, :] = total
        dec_src[layer : layer + 1, :] = total
        decays.append([(factor, jnp.sqrt(1.0 - factor * factor)) for factor in factors])

    @pl.when(is_owner)
    def _():
        dec_box[me] = dec_src[...]

    neighbours = has_up.astype(jnp.int32) + has_down.astype(jnp.int32)

    def meet():
        pl.semaphore_wait(
            barrier, jnp.where(is_owner, n - 1 + neighbours * n, owners + neighbours * (owners + 1))
        )

    def send_halo(layer, which, top, bottom):
        for d, (src, (there, other)) in enumerate(zip((top, bottom), sides)):
            send(there, src, halo.at[layer, which, 1 - d], halo_send.at[d],
                 halo_recv.at[layer, which, 1 - d], {"rows": other})

    def wait_halo(layer, which):
        for d, (there, _other) in enumerate(sides):
            received(there, halo.at[layer, which, d], halo_recv.at[layer, which, d])

    def spread(parts, count):
        size = count * frames * width
        column = lax.rem(lax.broadcasted_iota(jnp.int32, (size, parts[0].shape[1]), 0), width)
        left = jnp.where(column == 0, 0.0, pltpu.roll(parts[0], 1, 0))
        right = jnp.where(column == width - 1, 0.0, pltpu.roll(parts[2], size - 1, 0))
        return (parts[1] + left + right).reshape(count, frames, width, -1)

    def conv(x, weights, wanted):
        lhs = [jnp.concatenate([x(i + a - 1).reshape(frames * width, chans) for i in wanted], axis=0) for a in range(3)]
        lhs = jnp.concatenate(lhs, axis=1)
        parts = []
        for b in range(3):
            rhs = jnp.concatenate([weights(a, b) for a in range(3)], axis=0)
            parts.append(jnp.dot(lhs, rhs, preferred_element_type=F32))
        return spread(parts, len(wanted))

    def scan(layer, driven):
        states = []
        for t in range(frames):
            factor, gain = decays[layer][t]
            fresh = gain * driven[t]
            states.append(fresh if t == 0 else factor * states[-1] + fresh)
        return states

    def drive(x, layer, g):
        mine = groups[g]
        wanted = [-1] + mine if g == 0 else mine + [rows]
        nothing = jnp.zeros((frames, width, chans), BF16)
        driven = conv(lambda i: x(i) if 0 <= i < rows else nothing, lambda a, b: wbuf[layer, 0, a, b], wanted)
        for j, r in enumerate(wanted):
            states = scan(layer, driven[j])
            if 0 <= r < rows:
                for t in range(frames):
                    st[r, t] = states[t]
            slot = r - mine[0] if 0 <= r < rows else len(mine)
            for s in range(owners):
                fin[layer, g, s, slot] = fold(states[-1][s * share : (s + 1) * share]).astype(BF16)

    def send_fin(layer, g):
        count = len(groups[g])
        there, other = sides[g]
        for s in range(owners):
            @pl.when(me == base + s)
            def _():
                inbox[layer, g, me, :count] = fin[layer, g, s, :count]

            send(both(me < n - 1, there), fin.at[layer, g, s, count], xbox.at[layer, 1 - g, me],
                 cross_send.at[g], cross_recv.at[layer, 1 - g], {"tm": base + s, "rows": other})
            send(both(me < n - 1, me != base + s), fin.at[layer, g, s, :count], inbox.at[layer, g, me, :count],
                 fin_send.at[g], fin_recv.at[layer, g], {"tm": base + s})

    def own(layer, g):
        count = len(groups[g])
        there, other = sides[g]
        edge = 0 if g == 0 else count - 1

        @pl.when(is_owner)
        def _():
            for last, size in ((me < n - 1, n - 2), (me == n - 1, n - 1)):
                received(last, first(inbox, (layer, g), size, pl.ds(0, count)), fin_recv.at[layer, g])
                if layer == 0 and g == 0:
                    received(last, first(dec_box, (), size), dec_recv)
            received(there, first(xbox, (layer, g), n - 1), cross_recv.at[layer, g])
            total = None
            for k in range(1, n):
                last = unfold(inbox[layer, g, k - 1, :count].astype(F32))
                cross = unfold(xbox[layer, g, k - 1].astype(F32))
                last = jnp.stack([last[j] + cross if j == edge else last[j] for j in range(count)])
                total = last if total is None else dec_box[k - 1, layer : layer + 1, :] * total + last
                outbox[layer, g, k, :count] = fold(total).astype(BF16)
                send(there, outbox.at[layer, g, k, edge], hcarry.at[layer, 1 - g, my_share],
                     hcar_send.at[g], hcar_recv.at[layer, 1 - g], {"tm": k, "rows": other})
                send(me != k, outbox.at[layer, g, k, :count], carry.at[layer, g, my_share, :count],
                     car_send.at[g], car_recv.at[layer, g], {"tm": k})

            carry[layer, g, my_share, :count] = outbox[layer, g, me, :count]

    def complete(layer):
        wait_halo(layer, 0)
        for d in range(2):
            v = halo[layer, 0, d].reshape(frames * width, chans)
            parts = [jnp.dot(v, wbuf[layer, 0, 2 * d, b], preferred_element_type=F32) for b in range(3)]
            states = scan(layer, spread(parts, 1)[0])
            for t in range(frames):
                state = st[edge_row[d], t] + states[t]
                st[edge_row[d], t] = state
                sth[layer, d, t] = state.astype(BF16)
        send_halo(layer, 1, sth.at[layer, 0], sth.at[layer, 1])

    def finish(layer, g):
        count = len(groups[g])
        for cond, size in ((is_owner, owners - 1), (jnp.logical_not(is_owner), owners)):
            received(both(me > 0, cond), first(carry, (layer, g), size, pl.ds(0, count)), car_recv.at[layer, g])
        for j, r in enumerate(groups[g]):
            incoming = jnp.concatenate([unfold(carry[layer, g, s, j].astype(F32)) for s in range(owners)], axis=0)
            for t in range(frames):
                xs[layer, r, t] = (st[r, t] + cums[layer, t : t + 1, :] * incoming).astype(BF16)

    def finish_halo(layer):
        wait_halo(layer, 1)
        for d, (there, _other) in enumerate(sides):
            received(both(me > 0, there), hcarry.at[layer, d], hcar_recv.at[layer, d])
            incoming = jnp.concatenate([unfold(hcarry[layer, d, s].astype(F32)) for s in range(owners)], axis=0)
            for t in range(frames):
                local = halo[layer, 1, d, t].astype(F32)
                xh[layer, d, t] = (local + cums[layer, t : t + 1, :] * incoming).astype(BF16)

    def mix(x, layer, wanted, put):
        def states(i):
            return xh[layer, 0] if i < 0 else xh[layer, 1] if i == rows else xs[layer, i]

        mixed = conv(states, lambda a, b: wbuf[layer, 1, a, b], wanted)
        gain = feed[layer : layer + 1, :]
        for j, r in enumerate(wanted):
            skipped = x(r).astype(F32)
            put(r, gelu(mixed[j] + gain * skipped).astype(BF16))

    x = lambda r: x0[r]
    pltpu.make_async_copy(x0, x0, lat_sem).wait()
    for layer in range(layers):
        if layer == 0:
            w_copies[0, 0].wait()
            w_copies[0, 1].start()
            drive(x, layer, 0)
            meet()
            for s in range(owners):
                send(both(me < n - 1, me != base + s), dec_src, dec_box.at[me], dec_send,
                     dec_recv, {"tm": base + s})
            send_fin(layer, 0)
        else:
            w_copies[layer, 0].wait()
            drive(x, layer, 0)
            send_fin(layer, 0)
        drive(x, layer, 1)
        send_fin(layer, 1)
        if layer == 0:
            send_halo(0, 0, lat.at[:, 0], lat.at[:, rows - 1])
        else:
            send_halo(layer, 0, x1.at[layer - 1, 0], x1.at[layer - 1, rows - 1])
        if layer < layers - 1:
            w_copies[layer + 1, 0].start()
            w_copies[layer + 1, 1].start()
        complete(layer)
        for g in range(2):
            own(layer, g)
        for g in range(2):
            finish(layer, g)
        finish_halo(layer)
        w_copies[layer, 1].wait()
        if layer == layers - 1:
            def put(r, v):
                out[:, r] = v
        else:
            def put(r, v):
                x1[layer, r] = v

        mix(x, layer, list(range(rows)), put)
        x = functools.partial(lambda layer, r: x1[layer, r], layer)

    for cond, size in ((is_owner, owners - 1), (jnp.logical_not(is_owner), owners)):
        sent(both(me < n - 1, cond), first(dec_box, (), size), dec_send)
        for g in range(2):
            sent(both(me < n - 1, cond), first(fin, (slice(None), g), size, pl.ds(0, len(groups[g]))), fin_send.at[g])
    for g, (there, _other) in enumerate(sides):
        sent(there, halo.at[:, :, g], halo_send.at[g])
        sent(both(me < n - 1, there), fin.at[:, g, :, len(groups[g])], cross_send.at[g])
        sent(is_owner, first(outbox, (slice(None), g), n - 2, pl.ds(0, len(groups[g]))), car_send.at[g])
        sent(both(is_owner, there), outbox.at[:, g, pl.ds(0, n - 1), 0], hcar_send.at[g])


def per_device(n, bands, latents, frame_gaps, decay_rates, input_kernel, output_kernel, feedthrough):
    frames, rows, width, chans = latents.shape
    layers = input_kernel.shape[0]
    owners = min(n // 2, max(width // 8, 1))
    base = n // 2 - owners // 2
    share = width // owners
    most = rows - rows // 2
    hbm = pl.BlockSpec(memory_space=pltpu.HBM)
    vmem = pl.BlockSpec(memory_space=pltpu.VMEM)
    dma = pltpu.SemaphoreType.DMA
    return pl.pallas_call(
        functools.partial(kernel, n, bands, base, owners),
        out_shape=pltpu.VMEM(latents.shape, BF16),
        in_specs=[hbm] * 6,
        out_specs=vmem,
        scratch_shapes=[
            pltpu.SMEM((frames,), F32),
            pltpu.VMEM((layers, chans), F32),
            pltpu.VMEM((layers, chans), F32),
            pltpu.VMEM((rows, frames, width, chans), BF16),
            pltpu.VMEM((max(layers - 1, 1), rows, frames, width, chans), BF16),
            pltpu.VMEM((layers, rows, frames, width, chans), BF16),
            pltpu.VMEM((layers, 2, frames, width, chans), BF16),
            pltpu.VMEM((rows, frames, width, chans), F32),
            pltpu.VMEM((layers, 2, frames, width, chans), BF16),
            pltpu.VMEM((layers, 2, 2, frames, width, chans), BF16),
            pltpu.VMEM((layers, 2) + input_kernel.shape[1:], BF16),
            pltpu.VMEM((layers, frames, chans), F32),
            pltpu.VMEM((layers, chans), F32),
            pltpu.VMEM((n, layers, chans), F32),
            pltpu.VMEM((layers, 2, owners, most + 1, 2 * share, chans // 2), BF16),
            pltpu.VMEM((layers, 2, n, most, 2 * share, chans // 2), BF16),
            pltpu.VMEM((layers, 2, n, 2 * share, chans // 2), BF16),
            pltpu.VMEM((layers, 2, n, most, 2 * share, chans // 2), BF16),
            pltpu.VMEM((layers, 2, owners, most, 2 * share, chans // 2), BF16),
            pltpu.VMEM((layers, 2, owners, 2 * share, chans // 2), BF16),
            dma((3,)),
            dma,
            dma((layers, 2)),
            dma((2,)),
            dma((layers, 2, 2)),
            dma,
            dma,
            dma((2,)),
            dma((layers, 2)),
            dma((2,)),
            dma((layers, 2)),
            dma((2,)),
            dma((layers, 2)),
            dma((2,)),
            dma((layers, 2)),
        ],
        compiler_params=pltpu.CompilerParams(collective_id=0, has_side_effects=True, vmem_limit_bytes=60 * 1024 * 1024),
    )(latents, frame_gaps, decay_rates, feedthrough, input_kernel, output_kernel)


def solution(mesh):
    in_specs = (P("tm", "rows", None, None), P("tm"), P(), P(), P(), P())
    out_specs = P("tm", "rows", None, None)
    return jax.shard_map(
        functools.partial(per_device, mesh.shape["tm"], mesh.shape["rows"]),
        mesh=mesh, in_specs=in_specs, out_specs=out_specs, check_vma=False,
    )
```

```python
import functools

import jax
import jax.numpy as jnp
from jax import lax
from jax.experimental import pallas as pl
from jax.experimental.pallas import tpu as pltpu
from jax.sharding import PartitionSpec as P

MESH = pl.DeviceIdType.MESH
F32 = jnp.float32
BF16 = jnp.bfloat16


def gelu(v):
    return 0.5 * v * (1.0 + jnp.tanh(0.7978845608028654 * (v + 0.044715 * (v * v * v))))


def fold(v):
    half = v.shape[-1] // 2
    return jnp.concatenate([v[..., :half], v[..., half:]], axis=-2)


def unfold(v):
    half = v.shape[-2] // 2
    return jnp.concatenate([v[..., :half, :], v[..., half:, :]], axis=-1)


def kernel(
    n, bands, base, owners,
    lat, gaps_in, rates_in, feed_in, win, wout,
    out,
    gaps, rates, feed, x0, x1, xs, xh, st, sth, halo, wbuf, cums, dec_src, dec_box,
    fin, inbox, xbox, tot, outbox, carry, hcarry,
    small_sem, lat_sem, w_sem, halo_send, halo_recv, dec_send, dec_recv, fin_send, fin_recv, cross_send, cross_recv,
    car_send, car_recv, hcar_send, hcar_recv,
):
    layers = win.shape[0]
    frames, rows, width, chans = lat.shape
    share = width // owners
    me = lax.axis_index("tm")
    band = lax.axis_index("rows")
    has_up = band > 0
    has_down = band < bands - 1
    is_owner = jnp.logical_and(me >= base, me < base + owners)
    my_share = lax.rem(me + owners * n - base, owners)
    half = max(n // 2, 1)
    spans = [(0, half), (half, n - 1)]
    late = (me >= half).astype(jnp.int32)
    groups = [list(range(rows // 2)), list(range(rows // 2, rows))]
    sides = [(has_up, lax.rem(band + bands - 1, bands)), (has_down, lax.rem(band + 1, bands))]
    beyond_row = [-1, rows]
    edge_row = [0, rows - 1]

    def both(*conds):
        return functools.reduce(jnp.logical_and, conds)

    def send(cond, src, dst, ssem, rsem, dev):
        copy = pltpu.make_async_remote_copy(
            src_ref=src, dst_ref=dst, send_sem=ssem, recv_sem=rsem, device_id=dev, device_id_type=MESH
        )
        pl.when(cond)(copy.start)

    def waiter(ref, sem):
        return pltpu.make_async_remote_copy(
            src_ref=ref, dst_ref=ref, send_sem=sem, recv_sem=sem, device_id={"tm": 0}, device_id_type=MESH
        )

    def received(cond, ref, sem):
        if ref is not None:
            pl.when(cond)(lambda: waiter(ref, sem).wait_recv())

    def sent(cond, ref, sem):
        if ref is not None:
            pl.when(cond)(lambda: waiter(ref, sem).wait_send())

    def first(ref, lead, size, *rest):
        return ref.at[(*lead, pl.ds(0, size), *rest)] if size > 0 else None

    barrier = pltpu.get_barrier_semaphore()

    def greet(cond, dev):
        @pl.when(cond)
        def _():
            pl.semaphore_signal(barrier, inc=1, device_id=dev, device_id_type=MESH)

    small = [pltpu.make_async_copy(src, dst, small_sem.at[i])
             for i, (src, dst) in enumerate(((gaps_in, gaps), (rates_in, rates), (feed_in, feed)))]
    w_copies = {(layer, which): pltpu.make_async_copy(src.at[layer], wbuf.at[layer, which], w_sem.at[layer, which])
                for layer in range(layers) for which, src in enumerate((win, wout))}
    row_copies = [pltpu.make_async_copy(lat.at[:, r], x0.at[r], lat_sem) for r in range(rows)]

    for k in range(n):
        owns = base <= k < base + owners
        greet(me != k if owns else both(is_owner, me != k), {"tm": k})
    for copy in small:
        copy.start()
    w_copies[0, 0].start()
    for copy in row_copies:
        copy.start()
    for there, other in sides:
        for k in range(n):
            if base <= k < base + owners:
                greet(there, {"tm": k, "rows": other})
            else:
                greet(both(there, jnp.logical_or(is_owner, me == k)), {"tm": k, "rows": other})

    for d, (there, _other) in enumerate(sides):
        @pl.when(jnp.logical_not(there))
        def _():
            for layer in range(layers):
                for which in range(2):
                    halo[layer, which, d] = jnp.zeros(halo.shape[3:], BF16)
                xbox[layer, d] = jnp.zeros(xbox.shape[2:], BF16)

        @pl.when(jnp.logical_or(me == 0, jnp.logical_not(there)))
        def _():
            for layer in range(layers):
                hcarry[layer, d] = jnp.zeros(hcarry.shape[2:], BF16)

    @pl.when(me == 0)
    def _():
        carry[...] = jnp.zeros(carry.shape, BF16)

    for copy in small:
        copy.wait()
    decays = []
    for layer in range(layers):
        rate = rates[layer : layer + 1, :]
        factors = [jnp.exp(-gaps[t] * rate) for t in range(frames)]
        total = factors[0]
        cums[layer, 0:1, :] = total
        for t in range(1, frames):
            total = total * factors[t]
            cums[layer, t : t + 1, :] = total
        dec_src[layer : layer + 1, :] = total
        decays.append([(factor, jnp.sqrt(1.0 - factor * factor)) for factor in factors])

    @pl.when(is_owner)
    def _():
        dec_box[me] = dec_src[...]

    neighbours = has_up.astype(jnp.int32) + has_down.astype(jnp.int32)

    def meet():
        pl.semaphore_wait(
            barrier, jnp.where(is_owner, n - 1 + neighbours * n, owners + neighbours * (owners + 1))
        )

    def send_halo(layer, which, top, bottom):
        for d, (src, (there, other)) in enumerate(zip((top, bottom), sides)):
            send(there, src, halo.at[layer, which, 1 - d], halo_send.at[d],
                 halo_recv.at[layer, which, 1 - d], {"rows": other})

    def wait_halo(layer, which):
        for d, (there, _other) in enumerate(sides):
            received(there, halo.at[layer, which, d], halo_recv.at[layer, which, d])

    def spread(parts, count):
        size = count * frames * width
        column = lax.rem(lax.broadcasted_iota(jnp.int32, (size, parts[0].shape[1]), 0), width)
        left = jnp.where(column == 0, 0.0, pltpu.roll(parts[0], 1, 0))
        right = jnp.where(column == width - 1, 0.0, pltpu.roll(parts[2], size - 1, 0))
        return (parts[1] + left + right).reshape(count, frames, width, -1)

    def conv(x, weights, wanted):
        lhs = [jnp.concatenate([x(i + a - 1).reshape(frames * width, chans) for i in wanted], axis=0) for a in range(3)]
        lhs = jnp.concatenate(lhs, axis=1)
        parts = []
        for b in range(3):
            rhs = jnp.concatenate([weights(a, b) for a in range(3)], axis=0)
            parts.append(jnp.dot(lhs, rhs, preferred_element_type=F32))
        return spread(parts, len(wanted))

    def scan(layer, driven):
        states = []
        for t in range(frames):
            factor, gain = decays[layer][t]
            fresh = gain * driven[t]
            states.append(fresh if t == 0 else factor * states[-1] + fresh)
        return states

    def drive(x, layer, g):
        mine = groups[g]
        wanted = [-1] + mine if g == 0 else mine + [rows]
        nothing = jnp.zeros((frames, width, chans), BF16)
        driven = conv(lambda i: x(i) if 0 <= i < rows else nothing, lambda a, b: wbuf[layer, 0, a, b], wanted)
        for j, r in enumerate(wanted):
            states = scan(layer, driven[j])
            if 0 <= r < rows:
                for t in range(frames):
                    st[r, t] = states[t]
            slot = r - mine[0] if 0 <= r < rows else len(mine)
            for s in range(owners):
                fin[layer, g, s, slot] = fold(states[-1][s * share : (s + 1) * share]).astype(BF16)

    def send_fin(layer, g):
        count = len(groups[g])
        there, other = sides[g]
        for s in range(owners):
            @pl.when(me == base + s)
            def _():
                inbox[layer, g, me, :count] = fin[layer, g, s, :count]

            send(both(me < n - 1, there), fin.at[layer, g, s, count], xbox.at[layer, 1 - g, me],
                 cross_send.at[g], cross_recv.at[layer, 1 - g, late], {"tm": base + s, "rows": other})
            send(both(me < n - 1, me != base + s), fin.at[layer, g, s, :count], inbox.at[layer, g, me, :count],
                 fin_send.at[g], fin_recv.at[layer, g, late], {"tm": base + s})

    def own(layer, g, part):
        count = len(groups[g])
        there, other = sides[g]
        edge = 0 if g == 0 else count - 1
        low, high = spans[part]
        inside = both(me >= low, me < high)

        def gather():
            for mine, size in ((inside, high - low - 1), (jnp.logical_not(inside), high - low)):
                received(mine, first(inbox, (layer, g), size, pl.ds(0, count)), fin_recv.at[layer, g, part])
                if layer == 0 and g == 0:
                    received(mine, first(dec_box, (), size), dec_recv.at[part])
            received(there, first(xbox, (layer, g), high - low), cross_recv.at[layer, g, part])
            total = tot[g, :count] if part else None
            for k in range(low + 1, high + 1):
                last = unfold(inbox[layer, g, k - 1, :count].astype(F32))
                cross = unfold(xbox[layer, g, k - 1].astype(F32))
                last = jnp.stack([last[j] + cross if j == edge else last[j] for j in range(count)])
                total = last if total is None else dec_box[k - 1, layer : layer + 1, :] * total + last
                outbox[layer, g, k, :count] = fold(total).astype(BF16)
                send(there, outbox.at[layer, g, k, edge], hcarry.at[layer, 1 - g, my_share],
                     hcar_send.at[g], hcar_recv.at[layer, 1 - g], {"tm": k, "rows": other})
                send(me != k, outbox.at[layer, g, k, :count], carry.at[layer, g, my_share, :count],
                     car_send.at[g], car_recv.at[layer, g], {"tm": k})
            if part:
                carry[layer, g, my_share, :count] = outbox[layer, g, me, :count]
            else:
                tot[g, :count] = total

        pl.when(is_owner)(gather)

    def complete(layer):
        wait_halo(layer, 0)
        for d in range(2):
            v = halo[layer, 0, d].reshape(frames * width, chans)
            parts = [jnp.dot(v, wbuf[layer, 0, 2 * d, b], preferred_element_type=F32) for b in range(3)]
            states = scan(layer, spread(parts, 1)[0])
            for t in range(frames):
                state = st[edge_row[d], t] + states[t]
                st[edge_row[d], t] = state
                sth[layer, d, t] = state.astype(BF16)
        send_halo(layer, 1, sth.at[layer, 0], sth.at[layer, 1])

    def finish(layer, g):
        count = len(groups[g])
        for cond, size in ((is_owner, owners - 1), (jnp.logical_not(is_owner), owners)):
            received(both(me > 0, cond), first(carry, (layer, g), size, pl.ds(0, count)), car_recv.at[layer, g])
        for j, r in enumerate(groups[g]):
            incoming = jnp.concatenate([unfold(carry[layer, g, s, j].astype(F32)) for s in range(owners)], axis=0)
            for t in range(frames):
                xs[layer, r, t] = (st[r, t] + cums[layer, t : t + 1, :] * incoming).astype(BF16)

    def finish_halo(layer):
        wait_halo(layer, 1)
        for d, (there, _other) in enumerate(sides):
            received(both(me > 0, there), hcarry.at[layer, d], hcar_recv.at[layer, d])
            incoming = jnp.concatenate([unfold(hcarry[layer, d, s].astype(F32)) for s in range(owners)], axis=0)
            for t in range(frames):
                local = halo[layer, 1, d, t].astype(F32)
                xh[layer, d, t] = (local + cums[layer, t : t + 1, :] * incoming).astype(BF16)

    def mix(x, layer, wanted, put):
        def states(i):
            return xh[layer, 0] if i < 0 else xh[layer, 1] if i == rows else xs[layer, i]

        mixed = conv(states, lambda a, b: wbuf[layer, 1, a, b], wanted)
        gain = feed[layer : layer + 1, :]
        for j, r in enumerate(wanted):
            skipped = x(r).astype(F32)
            put(r, gelu(mixed[j] + gain * skipped).astype(BF16))

    x = lambda r: x0[r]
    pltpu.make_async_copy(x0, x0, lat_sem).wait()
    for layer in range(layers):
        if layer == 0:
            w_copies[0, 0].wait()
            w_copies[0, 1].start()
            drive(x, layer, 0)
            meet()
            for s in range(owners):
                send(both(me < n - 1, me != base + s), dec_src, dec_box.at[me], dec_send,
                     dec_recv.at[late], {"tm": base + s})
            send_fin(layer, 0)
        else:
            w_copies[layer, 0].wait()
            drive(x, layer, 0)
            send_fin(layer, 0)
        drive(x, layer, 1)
        send_fin(layer, 1)
        if layer == 0:
            send_halo(0, 0, lat.at[:, 0], lat.at[:, rows - 1])
        else:
            send_halo(layer, 0, x1.at[layer - 1, 0], x1.at[layer - 1, rows - 1])
        if layer < layers - 1:
            w_copies[layer + 1, 0].start()
            w_copies[layer + 1, 1].start()
        for g in range(2):
            own(layer, g, 0)
        complete(layer)
        for g in range(2):
            own(layer, g, 1)
        for g in range(2):
            finish(layer, g)
        finish_halo(layer)
        w_copies[layer, 1].wait()
        if layer == layers - 1:
            def put(r, v):
                out[:, r] = v
        else:
            def put(r, v):
                x1[layer, r] = v

        mix(x, layer, list(range(rows)), put)
        x = functools.partial(lambda layer, r: x1[layer, r], layer)

    for cond, size in ((is_owner, owners - 1), (jnp.logical_not(is_owner), owners)):
        sent(both(me < n - 1, cond), first(dec_box, (), size), dec_send)
        for g in range(2):
            sent(both(me < n - 1, cond), first(fin, (slice(None), g), size, pl.ds(0, len(groups[g]))), fin_send.at[g])
    for g, (there, _other) in enumerate(sides):
        sent(there, halo.at[:, :, g], halo_send.at[g])
        sent(both(me < n - 1, there), fin.at[:, g, :, len(groups[g])], cross_send.at[g])
        sent(is_owner, first(outbox, (slice(None), g), n - 2, pl.ds(0, len(groups[g]))), car_send.at[g])
        sent(both(is_owner, there), outbox.at[:, g, pl.ds(0, n - 1), 0], hcar_send.at[g])


def per_device(n, bands, latents, frame_gaps, decay_rates, input_kernel, output_kernel, feedthrough):
    frames, rows, width, chans = latents.shape
    layers = input_kernel.shape[0]
    owners = min(n // 2, max(width // 8, 1))
    base = n // 2 - owners // 2
    share = width // owners
    most = rows - rows // 2
    hbm = pl.BlockSpec(memory_space=pltpu.HBM)
    vmem = pl.BlockSpec(memory_space=pltpu.VMEM)
    dma = pltpu.SemaphoreType.DMA
    return pl.pallas_call(
        functools.partial(kernel, n, bands, base, owners),
        out_shape=pltpu.VMEM(latents.shape, BF16),
        in_specs=[hbm] * 6,
        out_specs=vmem,
        scratch_shapes=[
            pltpu.SMEM((frames,), F32),
            pltpu.VMEM((layers, chans), F32),
            pltpu.VMEM((layers, chans), F32),
            pltpu.VMEM((rows, frames, width, chans), BF16),
            pltpu.VMEM((max(layers - 1, 1), rows, frames, width, chans), BF16),
            pltpu.VMEM((layers, rows, frames, width, chans), BF16),
            pltpu.VMEM((layers, 2, frames, width, chans), BF16),
            pltpu.VMEM((rows, frames, width, chans), F32),
            pltpu.VMEM((layers, 2, frames, width, chans), BF16),
            pltpu.VMEM((layers, 2, 2, frames, width, chans), BF16),
            pltpu.VMEM((layers, 2) + input_kernel.shape[1:], BF16),
            pltpu.VMEM((layers, frames, chans), F32),
            pltpu.VMEM((layers, chans), F32),
            pltpu.VMEM((n, layers, chans), F32),
            pltpu.VMEM((layers, 2, owners, most + 1, 2 * share, chans // 2), BF16),
            pltpu.VMEM((layers, 2, n, most, 2 * share, chans // 2), BF16),
            pltpu.VMEM((layers, 2, n, 2 * share, chans // 2), BF16),
            pltpu.VMEM((2, most, share, chans), F32),
            pltpu.VMEM((layers, 2, n, most, 2 * share, chans // 2), BF16),
            pltpu.VMEM((layers, 2, owners, most, 2 * share, chans // 2), BF16),
            pltpu.VMEM((layers, 2, owners, 2 * share, chans // 2), BF16),
            dma((3,)),
            dma,
            dma((layers, 2)),
            dma((2,)),
            dma((layers, 2, 2)),
            dma,
            dma((2,)),
            dma((2,)),
            dma((layers, 2, 2)),
            dma((2,)),
            dma((layers, 2, 2)),
            dma((2,)),
            dma((layers, 2)),
            dma((2,)),
            dma((layers, 2)),
        ],
        compiler_params=pltpu.CompilerParams(collective_id=0, has_side_effects=True, vmem_limit_bytes=60 * 1024 * 1024),
    )(latents, frame_gaps, decay_rates, feedthrough, input_kernel, output_kernel)


def solution(mesh):
    in_specs = (P("tm", "rows", None, None), P("tm"), P(), P(), P(), P())
    out_specs = P("tm", "rows", None, None)
    return jax.shard_map(
        functools.partial(per_device, mesh.shape["tm"], mesh.shape["rows"]),
        mesh=mesh, in_specs=in_specs, out_specs=out_specs, check_vma=False,
    )
```
